32 devices in a mesh: narrow: 2 (over y), wide: 4 (over z), nys: 4 (over x, core).
Axes of the slice: x: 2, y: 2, z: 4, core: 2. Of those that a mesh axis runs over, the one named last changes fastest.
Arguments:
- centers: bfloat16 [32768, 1024], P(('narrow', 'wide', 'nys')), may hold values from -6 to 6
- weights: float32 [32768, 1000], P(('narrow', 'wide', 'nys')), may hold values from -6 to 6
- batch_points: bfloat16 [512, 1024], P(('narrow', 'wide', 'nys')), may hold values from -6 to 6
- labels: float32 [512, 1000], P(('narrow', 'wide', 'nys')), may hold values from -6 to 6
- nystrom_points: bfloat16 [2048, 1024], P(('narrow', 'nys')), may hold values from -6 to 6
- eigvecs: float32 [2048, 160], P(('narrow', 'nys')), may hold values from -0.125 to 0.125
- corrections: float32 [160], replicated, may hold values from 0.05 to 0.5
Outputs:
- new_weights: float32 [32768, 1000], P(('narrow', 'wide', 'nys'))
The draws below stay inside these ranges and needn't reach their ends.
All inputs are finite; a program needn't handle non-finite values.
Results may differ from the reference program's by a relative error of at most 0.0003.
The reference program's roundings to bfloat16 on the way (of `kernel`, `residual` and `corrected`) count: a program that leaves them out, or rounds other values in their place, can miss the bound.
Values may be sent and summed in bfloat16 or wider, within the bound.
No kernel may reach another device: no remote copies, remote signals or barrier semaphores. Data moves between devices by JAX's collectives and lax.ppermute only.
A program may use at most 64 MiB of HBM per device.

```python
import math
import jax
import jax.numpy as jnp
from jax import lax

D = 1024
OUT = 1000
Q = 160
NYS = 2048
BATCH = 512
CEN_DEV = 1024
CENTERS = 32768


twin_count = 8


def spread_rows(key, rows):
    return jax.random.normal(jax.random.fold_in(key, 1), (rows, D), jnp.float32)


def drawn(key):
    base = jax.random.normal(jax.random.fold_in(key, 11), (2 * twin_count, D), jnp.float32)
    return jnp.clip(2.0 * base, -6.0, 6.0)


def twin_rows(key, plants):
    sigma = (math.sqrt(2.0 * D) - 4.0) / math.sqrt(D)
    noise = jax.random.normal(key, plants.shape, jnp.float32)
    return plants + sigma * noise


def draw_centers(key, part):
    values = spread_rows(jax.random.fold_in(key, 21), CENTERS)
    order = jax.random.permutation(jax.random.fold_in(key, 22), CENTERS)[:2 * twin_count]
    values = values.at[order].set(drawn(key))
    return jnp.clip(values, -6.0, 6.0).astype(jnp.bfloat16)


def draw_batch_points(key, part):
    values = spread_rows(jax.random.fold_in(key, 31), BATCH)
    order = jax.random.permutation(jax.random.fold_in(key, 32), BATCH)[:twin_count]
    twins = twin_rows(jax.random.fold_in(key, 33), drawn(key)[:twin_count])
    values = values.at[order].set(twins)
    return jnp.clip(values, -6.0, 6.0).astype(jnp.bfloat16)


def draw_nystrom_points(key, part):
    values = spread_rows(jax.random.fold_in(key, 41), NYS)
    order = jax.random.permutation(jax.random.fold_in(key, 42), NYS)[:twin_count]
    twins = twin_rows(jax.random.fold_in(key, 43), drawn(key)[twin_count:])
    values = values.at[order].set(twins)
    return jnp.clip(values, -6.0, 6.0).astype(jnp.bfloat16)


def block_levels(own_key, shape, cuts, smallest, largest):
    factor_of = 1.0
    for dim, blocks in cuts:
        draws = jax.random.uniform(jax.random.fold_in(jax.random.fold_in(own_key, 6), dim), (blocks,), jnp.float32, smallest / len(cuts), largest / len(cuts))
        factor_of = factor_of * jnp.repeat(jnp.exp(draws), shape[dim] // blocks).reshape((-1,) + (1,) * (len(shape) - 1 - dim))
    return factor_of


def bell_draw(rng, extent, width, bound, pieces=(), dtype=jnp.bfloat16):
    array = width * jax.random.normal(rng, extent, jnp.float32)
    if pieces:
        array = array * block_levels(rng, extent, pieces, -0.22, 0.18)
    return jnp.clip(array, -bound, bound).astype(dtype)


def setup_inputs(seed: int = 0) -> dict:
    key_of = jax.random.split(jax.random.key(seed), 8)
    return {
        "centers": draw_centers(jax.random.fold_in(key_of[7], 71), 0),
        "weights": bell_draw(key_of[1], (CENTERS, OUT), 1.0, 6.0, ((0, 32),), jnp.float32),
        "batch_points": draw_batch_points(jax.random.fold_in(key_of[7], 71), 0),
        "labels": bell_draw(key_of[3], (BATCH, OUT), 1.0, 6.0, ((0, 32),), jnp.float32),
        "nystrom_points": draw_nystrom_points(jax.random.fold_in(key_of[7], 71), 0),
        "eigvecs": bell_draw(key_of[5], (NYS, Q), NYS ** -0.5, 0.125, ((0, 8),), jnp.float32),
        "corrections": jnp.clip(jnp.exp(jax.random.uniform(key_of[6], (Q,), jnp.float32, math.log(0.05), math.log(0.5))), 0.05, 0.5),
    }


RATE = 16.0
SPREAD = 4.0

def kernel(left, right):
    cross = lax.dot_general(left, right, (((1,), (1,)), ((), ())), preferred_element_type=jnp.float32)
    left_sq = lax.optimization_barrier(jnp.sum(jnp.square(left.astype(jnp.float32)), axis=1))
    right_sq = lax.optimization_barrier(jnp.sum(jnp.square(right.astype(jnp.float32)), axis=1))
    dist = jnp.sqrt(jnp.maximum(left_sq[:, None] + right_sq[None, :] - 2.0 * cross, 0.0))
    radius = math.sqrt(2.0 * left.shape[1])
    return jnp.exp((radius - dist) / SPREAD).astype(jnp.bfloat16)

def reference(centers, weights, batch_points, labels, nystrom_points, eigvecs, corrections):
    blocks_c = centers.reshape(-1, CEN_DEV, D)
    blocks_w = weights.reshape(-1, CEN_DEV, OUT)

    def accumulate(total, pair):
        block_c, block_w = pair
        tile = kernel(block_c, batch_points)
        term = lax.dot_general(tile, block_w.astype(jnp.bfloat16), (((0,), (0,)), ((), ())), preferred_element_type=jnp.float32)
        return (total + term, None)
    total, _ = lax.scan(accumulate, jnp.zeros((BATCH, OUT), jnp.float32), (blocks_c, blocks_w))
    predicted = total * CENTERS ** (-0.5)
    residual = (predicted - labels).astype(jnp.bfloat16)
    pulled = jnp.dot(kernel(nystrom_points, batch_points), residual, preferred_element_type=jnp.float32)
    projected = lax.dot_general(eigvecs, pulled, (((0,), (0,)), ((), ())), precision=lax.Precision.HIGHEST)
    corrected = jnp.dot(eigvecs, corrections[:, None] * projected, precision=lax.Precision.HIGHEST).astype(jnp.bfloat16)

    def update(pair):
        block_c, block_w = pair
        gradient = jnp.dot(kernel(block_c, batch_points), residual, preferred_element_type=jnp.float32)
        nystrom_term = jnp.dot(kernel(block_c, nystrom_points), corrected, preferred_element_type=jnp.float32)
        return block_w - RATE / BATCH * (gradient - nystrom_term)
    return lax.map(update, (blocks_c, blocks_w)).reshape(CENTERS, OUT)
```

```python
import functools
import itertools
import math

import jax
import jax.numpy as jnp
from jax import lax
from jax.experimental import pallas as pl
from jax.experimental.pallas import tpu as pltpu
from jax.sharding import PartitionSpec as P


RATE = 16.0
SPREAD = 4.0
AXES = ("narrow", "wide", "nys")
MIB = 1 << 20


def row_squares(points):
    return jnp.sum(jnp.square(points.astype(jnp.float32)), axis=1, keepdims=True)


def turned_row(column):
    return jnp.broadcast_to(column, (column.shape[0], 128)).T[:1]


def kernel_tile(left, right, right_sq):
    cross = lax.dot_general(
        left, right, (((1,), (1,)), ((), ())), preferred_element_type=jnp.float32
    )
    left_sq = row_squares(left)
    dist = jnp.sqrt(jnp.maximum(left_sq + right_sq - 2.0 * cross, 0.0))
    radius = math.sqrt(2.0 * left.shape[1])
    return jnp.exp((radius - dist) / SPREAD).astype(jnp.bfloat16)


def split3(value):
    high = value.astype(jnp.bfloat16)
    rest = value - high.astype(jnp.float32)
    mid = rest.astype(jnp.bfloat16)
    low = (rest - mid.astype(jnp.float32)).astype(jnp.bfloat16)
    return high, mid, low


def call(body, outs, *args, flops=0, exps=0, limit=None):
    size = lambda a: math.prod(a.shape) * a.dtype.itemsize
    moved = sum(map(size, args)) + sum(map(size, outs))
    single = len(outs) == 1
    vmem = pl.BlockSpec(memory_space=pltpu.VMEM)
    return pl.pallas_call(
        body,
        out_shape=outs[0] if single else tuple(outs),
        in_specs=[vmem] * len(args),
        out_specs=vmem if single else tuple([vmem] * len(outs)),
        compiler_params=pltpu.CompilerParams(vmem_limit_bytes=limit or moved + 2 * MIB),
        cost_estimate=pl.CostEstimate(
            flops=flops, bytes_accessed=moved, transcendentals=exps
        ),
    )(*args)


def shape(dims, dtype=jnp.float32):
    return jax.ShapeDtypeStruct(tuple(dims), dtype)


def join_body(*refs):
    out, start = refs[-1], 0
    for ref in refs[:-1]:
        out[start : start + ref.shape[0]] = ref[...]
        start += ref.shape[0]


def join(pieces):
    if len(pieces) == 1:
        return pieces[0]
    rows = sum(p.shape[0] for p in pieces)
    out = shape((rows,) + pieces[0].shape[1:], pieces[0].dtype)
    return call(join_body, [out], *pieces)


def sum_body(count, *refs):
    start = 0
    for out in refs[count:]:
        rows = out.shape[0]
        total = refs[0][start : start + rows]
        for ref in refs[1:count]:
            total = total + ref[start : start + rows]
        out[...] = total
        start += rows


def residual_body(scale, count, *refs):
    total = refs[0][...]
    for ref in refs[1:count]:
        total = total + ref[...]
    labels, out = refs[count:]
    outs = labels.shape[1]
    out[...] = jnp.zeros_like(out)
    out[:, :outs] = (total[:, :outs] * scale - labels[...]).astype(jnp.bfloat16)


def prep_body(weights, centers, corrections, weights_low, centers_sq, factors):
    outs = weights.shape[0]
    weights_low[:outs] = weights[...].astype(jnp.bfloat16)
    if weights_low.shape[0] > outs:
        weights_low[outs:] = jnp.zeros_like(weights_low[outs:])
    centers_sq[...] = turned_row(row_squares(centers[...]))
    q = corrections.shape[1]
    factors[...] = jnp.broadcast_to(corrections[...], (128, q)).T


def tile_body(start, kept, valued, *refs):
    refs = list(refs)
    points, centers, centers_sq = refs[:3]
    weights = refs[3] if valued else None
    scratch, sem = refs[-2:]
    tail = refs[-2 - (1 + kept + valued) : -2]
    tile = kernel_tile(points[...], centers[...], centers_sq[...])
    scratch[...] = tile
    copy = pltpu.make_async_copy(
        scratch, tail[0].at[pl.ds(start, points.shape[0])], sem
    )
    copy.start()
    if kept:
        tail[1][...] = tile
    if valued:
        tail[-1][...] = lax.dot_general(
            tile, weights[...], (((1,), (1,)), ((), ())), preferred_element_type=jnp.float32
        )
    copy.wait()


def tile_call(points, centers, centers_sq, buffer, start, total, kept=False, weights=None):
    n, features = points.shape
    n_centers = centers.shape[0]
    vmem = pl.BlockSpec(memory_space=pltpu.VMEM)
    hbm = pl.BlockSpec(memory_space=pl.ANY)
    args = [points, centers, centers_sq]
    specs = [vmem] * 3
    outs = [shape((total, n_centers), jnp.bfloat16)]
    flops = 2 * n * n_centers * features
    if kept:
        outs.append(shape((n, n_centers), jnp.bfloat16))
    if weights is not None:
        args.append(weights)
        specs.append(vmem)
        outs.append(shape((n, weights.shape[0])))
        flops += 2 * n * n_centers * weights.shape[0]
    alias = {}
    if buffer is not None:
        alias = {len(args): 0}
        args.append(buffer)
        specs.append(hbm)
    got = pl.pallas_call(
        functools.partial(tile_body, start, kept, weights is not None),
        out_shape=tuple(outs),
        in_specs=specs,
        out_specs=tuple([hbm] + [vmem] * (len(outs) - 1)),
        scratch_shapes=[pltpu.VMEM((n, n_centers), jnp.bfloat16), pltpu.SemaphoreType.DMA],
        input_output_aliases=alias,
        compiler_params=pltpu.CompilerParams(vmem_limit_bytes=9 * MIB),
        cost_estimate=pl.CostEstimate(
            flops=flops, bytes_accessed=4 * MIB, transcendentals=2 * n * n_centers
        ),
        name="tile",
    )(*args)
    return got if len(got) > 1 else got[0]


def value_body(tile, weights, value):
    value[...] = lax.dot_general(
        tile[...], weights[...], (((1,), (1,)), ((), ())), preferred_element_type=jnp.float32
    )


def pull_body(halves, count, last, *refs):
    refs = list(refs)
    batch, refs = refs[:halves], refs[halves:]
    points, vectors = refs[:count], refs[count : 2 * count]
    before = refs[2 * count] if last else None
    batch_sq = [turned_row(row_squares(b[...])) for b in batch]
    out, stack, tiles, parts = refs[-4:]
    q = vectors[0].shape[0]
    rows = batch[0].shape[0]
    start = 0
    for p, v in zip(points, vectors):
        n = p.shape[0]
        for k, part in enumerate(split3(v[...])):
            parts[k * q : (k + 1) * q, start : start + n] = part
        for k, i in enumerate((2, 1, 0, 1, 0, 0)):
            stack[k * q : (k + 1) * q, start : start + n] = parts[
                i * q : (i + 1) * q, start : start + n
            ]
        for h in range(halves):
            tiles[start : start + n, h * rows : (h + 1) * rows] = kernel_tile(
                p[...], batch[h][...], batch_sq[h]
            )
        start += n
    total = jnp.dot(parts[...], tiles[...], preferred_element_type=jnp.float32)
    total = total[2 * q :] + total[q : 2 * q] + total[:q]
    if before is not None:
        total = total + before[...]
    if out.dtype == jnp.bfloat16:
        for k, part in enumerate(split3(total)):
            out[k * q : (k + 1) * q] = part
    else:
        out[...] = total


def update_body(rate, halves, groups, *refs):
    refs = list(refs)
    residuals, pulling, factors = refs[:halves], refs[halves], refs[halves + 1]
    stacks = refs[halves + 2 : halves + 2 + groups]
    buffer, weights = refs[halves + 2 + groups : halves + 4 + groups]
    out, stack_v, buffer_v, weights_v, mixed, turned, sems, out_sems = refs[halves + 4 + groups :]
    outs, _ = weights.shape
    q = factors.shape[0]
    rows = residuals[0].shape[0]
    batch = halves * rows
    wide = stacks[0].shape[1]
    copies = [
        pltpu.make_async_copy(s, stack_v.at[:, pl.ds(i * wide, wide)], sems.at[i])
        for i, s in enumerate(stacks)
    ]
    copies.append(pltpu.make_async_copy(buffer, buffer_v, sems.at[groups]))
    copies.append(pltpu.make_async_copy(weights, weights_v, sems.at[groups + 1]))
    for copy in copies:
        copy.start()

    projected = None
    for h, r in enumerate(residuals):
        term = jnp.dot(
            pulling[:, h * rows : (h + 1) * rows], r[...], preferred_element_type=jnp.float32
        )
        projected = term if projected is None else projected + term
        turned[:, h * rows : (h + 1) * rows] = r[...].T
    projected = projected[2 * q :] + projected[q : 2 * q] + projected[:q]
    parts = split3(factors[:, :1] * projected)
    for k, i in enumerate((0, 1, 2, 0, 1, 0)):
        mixed[k * q : (k + 1) * q] = parts[i]

    for i in range(groups):
        copies[i].wait()
        corrected = lax.dot_general(
            mixed[...],
            stack_v[:, i * wide : (i + 1) * wide],
            (((0,), (0,)), ((), ())),
            preferred_element_type=jnp.float32,
        )
        turned[:, batch + i * wide : batch + (i + 1) * wide] = (-corrected).astype(jnp.bfloat16)
    copies[groups].wait()
    copies[groups + 1].wait()
    block = 256
    stores = []
    for i, start in enumerate(range(0, outs, block)):
        n = min(block, outs - start)
        total = jnp.dot(
            turned[start : start + n], buffer_v[...], preferred_element_type=jnp.float32
        )
        weights_v[start : start + n] = weights_v[start : start + n] - rate * total
        store = pltpu.make_async_copy(
            weights_v.at[pl.ds(start, n)], out.at[pl.ds(start, n)], out_sems.at[i]
        )
        store.start()
        stores.append(store)
    for store in stores:
        store.wait()


class Digits:
    def __init__(self, mesh):
        narrow, wide, nys = (mesh.shape[a] for a in AXES)
        pair = 2 if nys % 2 == 0 else 1
        self.sizes = (narrow, wide, nys // pair, pair)

    def perm(self, offsets):
        pairs = []
        for target in itertools.product(*(range(s) for s in self.sizes)):
            source = [(t + o) % s for t, o, s in zip(target, offsets, self.sizes)]
            pairs.append((self.flat(source), self.flat(target)))
        return pairs

    def flat(self, digits):
        index = 0
        for d, s in zip(digits, self.sizes):
            index = index * s + d
        return index

    def steps(self, dims):
        ranges = [range(s) if i in dims else (0,) for i, s in enumerate(self.sizes)]
        return list(itertools.product(*ranges))

    def fetch(self, value, offsets):
        if not any(offsets):
            return value
        return lax.ppermute(value, AXES, self.perm(offsets))

    def gather(self, value, dims):
        return [self.fetch(value, step) for step in self.steps(dims)]

    def scatter(self, pieces, dims):
        out = []
        for piece, step in zip(pieces, self.steps(dims)):
            back = tuple((s - o) % s for o, s in zip(step, self.sizes))
            out.append(self.fetch(piece, back))
        return out


def chunks(pieces, rows, axis=0):
    size = pieces[0].shape[axis]
    many = max(1, rows // size)
    groups = [pieces[i : i + many] for i in range(0, len(pieces), many)]
    if many == 1:
        return pieces
    return [jnp.concatenate(g, axis=axis) for g in groups]


def per_device(digits, centers, weights, batch_points, labels, nystrom_points, eigvecs, corrections):
    count = math.prod(digits.sizes)
    scale = (centers.shape[0] * count) ** (-0.5)
    batch = labels.shape[0] * count
    plane, line, pair = (0, 2), (1,), (3,)
    halves = digits.sizes[3]
    rows = batch // halves
    n_centers, features = centers.shape
    outs = weights.shape[1]
    padded = pl.cdiv(outs, 128) * 128
    q = eigvecs.shape[1]
    nys = nystrom_points.shape[0] * digits.sizes[0] * digits.sizes[2] * halves
    total = batch + nys

    pieces = digits.gather(batch_points, line)
    piece = join(pieces)
    pieces = digits.gather(piece, plane)
    batch_own = join(pieces)
    batch_half = digits.gather(batch_own, pair)

    points_own = digits.gather(nystrom_points, plane)
    vectors_own = digits.gather(eigvecs.T, plane)
    points_own = chunks(points_own, 256)
    vectors_own = chunks(vectors_own, 256, axis=1)
    points = [digits.gather(p, pair) for p in points_own]
    vectors = [digits.gather(v, pair) for v in vectors_own]
    points = [[p[h] for p in points] for h in range(halves)]
    vectors = [[v[h] for v in vectors] for h in range(halves)]

    weights_t = weights.T
    weights_low, centers_sq, factors = call(
        prep_body,
        [
            shape((padded, n_centers), jnp.bfloat16),
            shape((1, n_centers)),
            shape((q, 128)),
        ],
        weights_t,
        centers,
        corrections[None, :],
        flops=4 * n_centers * features,
    )

    ordered = [p for group in points for p in group]
    buffer = tile_call(ordered[0], centers, centers_sq, None, batch, total)

    values = [None] * halves
    buffer, k_first = tile_call(batch_half[0], centers, centers_sq, buffer, 0, total, kept=True)
    for h in range(1, halves):
        buffer, values[h] = tile_call(
            batch_half[h], centers, centers_sq, buffer, h * rows, total, weights=weights_low
        )
    values[0] = call(
        value_body, [shape((rows, padded))], k_first, weights_low, flops=2 * rows * n_centers * outs
    )
    for dims, after in ((pair, plane), (plane, line)):
        values = digits.scatter(values, dims)
        cuts = len(digits.steps(after))
        cut = shape((values[0].shape[0] // cuts, padded))
        values = call(functools.partial(sum_body, len(values)), [cut] * cuts, *values)
        values = [values] if cuts == 1 else list(values)
    values = digits.scatter(values, line)
    residual = call(
        functools.partial(residual_body, scale, len(values)),
        [shape((labels.shape[0], padded), jnp.bfloat16)],
        *values,
        labels,
    )
    pieces = digits.gather(residual, line)
    residual = join(pieces)
    pieces = digits.gather(residual, plane)
    residual = join(pieces)
    residual = digits.gather(residual, pair)

    start = batch
    for i, p in enumerate(ordered):
        if i:
            buffer = tile_call(p, centers, centers_sq, buffer, start, total)
        start += p.shape[0]
    pulling, stacks = None, []
    for h in range(halves):
        last = h == halves - 1
        n = sum(p.shape[0] for p in points[h])
        some = [*batch_half, *points[h], *vectors[h]]
        if h:
            some.append(pulling)
        pulling, stack = pl.pallas_call(
            functools.partial(pull_body, halves, len(points[h]), h > 0),
            out_shape=(
                shape((3 * q, batch), jnp.bfloat16) if last else shape((q, batch)),
                shape((6 * q, n), jnp.bfloat16),
            ),
            in_specs=[pl.BlockSpec(memory_space=pltpu.VMEM)] * len(some),
            out_specs=(pl.BlockSpec(memory_space=pltpu.VMEM),) * 2,
            scratch_shapes=[
                pltpu.VMEM((n, batch), jnp.bfloat16),
                pltpu.VMEM((3 * q, n), jnp.bfloat16),
            ],
            compiler_params=pltpu.CompilerParams(vmem_limit_bytes=16 * MIB),
            cost_estimate=pl.CostEstimate(
                flops=2 * n * batch * (features + 3 * q),
                bytes_accessed=8 * MIB,
                transcendentals=2 * n * batch,
            ),
            name="pull",
        )(*some)
        stacks.append(stack)

    vmem = pl.BlockSpec(memory_space=pltpu.VMEM)
    hbm = pl.BlockSpec(memory_space=pl.ANY)
    new_t = pl.pallas_call(
        functools.partial(update_body, RATE / batch, halves, len(stacks)),
        out_shape=shape((outs, n_centers)),
        in_specs=[vmem] * (halves + 2) + [hbm] * (len(stacks) + 2),
        out_specs=hbm,
        scratch_shapes=[
            pltpu.VMEM((6 * q, nys), jnp.bfloat16),
            pltpu.VMEM((total, n_centers), jnp.bfloat16),
            pltpu.VMEM((outs, n_centers), jnp.float32),
            pltpu.VMEM((6 * q, padded), jnp.bfloat16),
            pltpu.VMEM((padded, total), jnp.bfloat16),
            pltpu.SemaphoreType.DMA((len(stacks) + 2,)),
            pltpu.SemaphoreType.DMA((pl.cdiv(outs, 256),)),
        ],
        compiler_params=pltpu.CompilerParams(vmem_limit_bytes=30 * MIB),
        cost_estimate=pl.CostEstimate(
            flops=2 * outs * (6 * q * nys + total * n_centers),
            bytes_accessed=24 * MIB,
            transcendentals=0,
        ),
        name="update",
    )(*residual, pulling, factors, *stacks, buffer, weights_t)
    return new_t.T


def solution(mesh):
    digits = Digits(mesh)
    rows = P(AXES, None)
    shared = P(("narrow", "nys"), None)

    def step(*args):
        return per_device(digits, *args)

    return jax.shard_map(
        step,
        mesh=mesh,
        in_specs=(rows, rows, rows, rows, shared, shared, P()),
        out_specs=rows,
        check_vma=False,
    )
```
